32 devices in a mesh: groups: 2 (over y), ep: 16 (over z, x, core).
Axes of the slice: x: 2, y: 2, z: 4, core: 2. Of those that a mesh axis runs over, the one named last changes fastest.
Arguments:
- tokens: bfloat16 [2048, 2880], P(('groups', 'ep')), parts along dimension 0, may hold values from -6 to 6
- expert_ids: int32 [2048, 4], P(('groups', 'ep')), parts along dimension 0, may hold values from 0 to 15, all different within a row; in each aligned block of 64 rows (0 to 63, 64 to 127, ...) at most 18 rows name the same one
- gate_ints: int32 [2048, 4], P(('groups', 'ep')), parts along dimension 0, may hold values from 1 to 255
- norm_gain: float32 [2880], replicated, may hold values from 0.5 to 2
- weight_in: bfloat16 [16, 2880, 5760], P('ep'), may hold values from -0.109375 to 0.109375
- bias_in: float32 [16, 5760], P('ep'), may hold values from -3 to 3
- weight_out: bfloat16 [16, 2880, 2880], P('ep'), may hold values from -0.109375 to 0.109375
- bias_out: float32 [16, 2880], replicated, may hold values from -3 to 3
Outputs:
- mixed: bfloat16 [2048, 2880], P(('groups', 'ep')), parts along dimension 0
The draws below stay inside these ranges and needn't reach their ends.
There are 2 independent parts, one for each index of `groups`. The reference program is written for one: setup_inputs(seed, part) draws one part's arguments, and reference() takes and returns one part's arrays. A program takes and returns all parts, laid end to end along the dimension named above; an argument that names none is the same for every part. Nothing has to cross between parts.
Inputs may be any that keep to these rules, and one draw needn't show every extreme that they name: `expert_ids`: each row names 4 different experts. Within the rows of one device (aligned blocks of 64 rows) no expert is named more than 18 times.
All inputs are finite; a program needn't handle non-finite values.
Results may differ from the reference program's by a relative error of at most 0.0065.
Values may be sent and summed in bfloat16 or wider, within the bound.
A program may use at most 256 MiB of HBM per device.

```python
import math
import jax
import jax.numpy as jnp
import numpy as np
from jax import lax

D = 2880
FF = 2880
EXPERTS = 16
TOPK = 4
ROWS_DEV = 64
CAP = 18
PARTS_SIZE = 1
PART_FF = 2880
ROWS = 1024
N_EP = 16


def touch_ends(result, stream_key, smallest, top_value):
    shape = result.shape
    place = [jax.random.randint(jax.random.fold_in(stream_key, axis), (), 0, shape[axis]) for axis in range(len(shape))]
    result = result.at[tuple(place)].set(smallest)
    longest = shape.index(max(shape))
    place[longest] = (place[longest] + 1) % shape[longest]
    return result.at[tuple(place)].set(top_value)


def block_levels(stream_key, dims, split, least, high):
    gain, own = 1.0, jax.random.fold_in(stream_key, 6)
    for axis_at, parts in split:
        heights = jnp.exp(jax.random.uniform(jax.random.fold_in(own, axis_at), (parts,), jnp.float32, least / len(split), high / len(split)))
        gain = gain * jnp.repeat(heights, dims[axis_at] // parts).reshape([-1 if axis == axis_at else 1 for axis in range(len(dims))])
    return gain


def routed_block(key, own, number, rows, amount, top, most, slope):
    sequence = jax.random.permutation(key, amount)
    packed, common = portions_of(amount, rows * top, most, slope, True), portions_of(amount, rows * top, most, slope, False)
    places = jnp.arange(amount)

    def named(tallies, rotation):
        used = int((tallies > 0).sum())
        fixed = max(1, used // 4)
        shifted = fixed + (places - fixed + rotation * (used - fixed)) % max(1, amount - fixed)
        return jnp.zeros((amount,), jnp.int32).at[sequence[jnp.where(places < fixed, places, shifted)]].set(jnp.asarray(tallies, jnp.int32))

    tallies = jnp.where(number % 4 == 0, named(packed, number // 4), named(common, number - number // 4 - 1))
    mixed = jax.random.permutation(jax.random.fold_in(own, 3), amount)
    source_of, sink = mixed[0:amount // 2 * 2:2], mixed[1:amount // 2 * 2:2]
    slack = jnp.minimum(tallies[source_of] - 1, most - tallies[sink]) // 2
    slack = jnp.where((source_of == sequence[0]) | (sink == sequence[0]) | (tallies[sink] == 0), 0, jnp.maximum(slack, 0))
    shifted = jax.random.randint(jax.random.fold_in(own, 4), (amount // 2,), 0, 1 << 20) % (slack + 1)
    tallies = tallies.at[source_of].add(-shifted).at[sink].add(shifted)
    labels = jnp.searchsorted(jnp.cumsum(tallies), jnp.arange(rows * top), side="right").astype(jnp.int32)
    table = labels.reshape(top, rows).T
    table = table[jax.random.permutation(jax.random.fold_in(own, 1), rows)]
    rotation = jax.random.randint(jax.random.fold_in(own, 2), (rows, 1), 0, top)
    return jnp.take_along_axis(table, (jnp.arange(top)[None, :] + rotation) % top, axis=1)


def portions_of(number_of, total, bound, skew, full):
    loads = [(1 << 20) // math.isqrt(grade ** skew) + 1 for grade in range(1, number_of + 1)]
    largest = bound if full else min(bound, max(-(-total // number_of), total * loads[0] // sum(loads)))
    least = 1 if total - largest >= number_of - 1 else 0
    given, surplus = [largest] + [least] * (number_of - 1), total - largest - least * (number_of - 1)
    while surplus > 0:
        candidates = [i for i in range(1, number_of) if given[i] < largest] or [i for i in range(1, number_of) if given[i] < bound]
        mass, left = sum([loads[i] for i in candidates]), surplus
        for i in candidates:
            extra = min(bound - given[i], max(1, left * loads[i] // mass), surplus)
            given[i] = given[i] + extra
            surplus = surplus - extra
    return np.array(given)


def gaussian(rng, extent, scale, reach, pieces=(), held_as=jnp.bfloat16):
    gain = block_levels(rng, extent, pieces, -0.22, 0.18) if pieces else 1.0
    array = jax.random.normal(rng, extent, jnp.float32) * scale * gain
    return jnp.minimum(jnp.maximum(array, -reach), reach).astype(held_as)


def setup_inputs(seed: int = 0, part: int = 0) -> dict:
    key_of = jax.random.split(jax.random.key(seed), 9)
    part_keys = jax.random.split(jax.random.fold_in(key_of[8], part), 9)
    tokens = gaussian(part_keys[0], (ROWS, D), 1.0, 6.0, ((0, 16),))
    expert_ids_keys = jax.random.split(jax.random.fold_in(part_keys[1], 1), ROWS // ROWS_DEV)
    expert_ids_turns = jax.random.permutation(jax.random.fold_in(part_keys[1], 3), ROWS // ROWS_DEV)
    expert_ids = jax.vmap(lambda own, number: routed_block(jax.random.fold_in(part_keys[1], 2), own, number, ROWS_DEV, EXPERTS, TOPK, CAP, 0))(expert_ids_keys, expert_ids_turns).reshape((ROWS, TOPK))
    gate_ints = touch_ends(jax.random.randint(part_keys[2], (ROWS, TOPK), 1, 256), jax.random.fold_in(part_keys[2], 1), 1, 255).astype(jnp.int32)
    norm_gain = jnp.clip(jnp.exp(jax.random.uniform(key_of[3], (D,), jnp.float32, math.log(0.5), math.log(2.0))), 0.5, 2.0)
    weight_in = gaussian(key_of[4], (EXPERTS * PARTS_SIZE, D, 2 * PART_FF), D ** -0.5, 0.109375, ((0, 16),))
    bias_in = gaussian(key_of[5], (EXPERTS * PARTS_SIZE, 2 * PART_FF), 0.5, 3.0, ((0, 16),), jnp.float32)
    weight_out = gaussian(key_of[6], (EXPERTS * PARTS_SIZE, PART_FF, D), FF ** -0.5, 0.109375, ((0, 16),))
    bias_out = gaussian(key_of[7], (EXPERTS, D), 0.5, 3.0, (), jnp.float32)
    return dict(tokens=tokens, expert_ids=expert_ids, gate_ints=gate_ints, norm_gain=norm_gain, weight_in=weight_in, bias_in=bias_in, weight_out=weight_out, bias_out=bias_out)


def swish_glu(pre_act, half_width):
    gate_part = pre_act[:, :half_width]
    up_part = pre_act[:, half_width:]
    return gate_part * jax.nn.sigmoid(1.702 * gate_part) * (up_part + 1.0)

def slot_tables(expert_ids, route_weight):
    entry_count = ROWS_DEV * TOPK
    flat_ids = expert_ids.reshape(N_EP, entry_count)
    one_hot = (flat_ids[:, :, None] == jnp.arange(EXPERTS, dtype=jnp.int32)[None, None, :]).astype(jnp.int32)
    earlier = jnp.cumsum(one_hot, axis=1) - one_hot
    slot_rank = lax.optimization_barrier(jnp.sum(earlier * one_hot, axis=2))
    slot_target = flat_ids * CAP + slot_rank
    source_dev = jnp.arange(N_EP, dtype=jnp.int32)[:, None] * jnp.ones((1, entry_count), jnp.int32)
    row_index = source_dev * ROWS_DEV + jnp.arange(entry_count, dtype=jnp.int32)[None, :] // TOPK
    row_table = jnp.full((N_EP, EXPERTS * CAP), -1, jnp.int32).at[source_dev, slot_target].set(row_index)
    weight_table = jnp.zeros((N_EP, EXPERTS * CAP), jnp.float32).at[source_dev, slot_target].set(route_weight.reshape(N_EP, entry_count))
    return (row_table.reshape(N_EP, EXPERTS, CAP), weight_table.reshape(N_EP, EXPERTS, CAP))

def reference(tokens, expert_ids, gate_ints, norm_gain, weight_in, bias_in, weight_out, bias_out):
    tok_float = tokens.astype(jnp.float32)
    row_scale = lax.rsqrt(lax.optimization_barrier(jnp.mean(tok_float * tok_float, axis=1, keepdims=True)) + 1e-05)
    normed = (tok_float * row_scale * norm_gain[None, :]).astype(jnp.bfloat16)
    int_gates = gate_ints.astype(jnp.float32)
    route_weight = int_gates / lax.optimization_barrier(jnp.sum(int_gates, axis=1, keepdims=True))
    row_table, weight_table = slot_tables(expert_ids, route_weight)

    def one_expert(running, expert_index):
        row_list = lax.dynamic_index_in_dim(row_table, expert_index, 1, keepdims=False).reshape(N_EP * CAP)
        slot_weight = lax.dynamic_index_in_dim(weight_table, expert_index, 1, keepdims=False).reshape(N_EP * CAP)
        safe_rows = jnp.maximum(row_list, 0)
        picked_rows = normed[safe_rows]
        part_sum = jnp.zeros((N_EP * CAP, D), jnp.float32)
        for part_index in range(PARTS_SIZE):
            weight_index = expert_index * PARTS_SIZE + part_index
            w_first = lax.dynamic_index_in_dim(weight_in, weight_index, 0, keepdims=False)
            b_first = lax.dynamic_index_in_dim(bias_in, weight_index, 0, keepdims=False)
            pre_act = jnp.dot(picked_rows, w_first, preferred_element_type=jnp.float32) + b_first[None, :]
            activated = swish_glu(pre_act, PART_FF).astype(jnp.bfloat16)
            w_second = lax.dynamic_index_in_dim(weight_out, weight_index, 0, keepdims=False)
            partial_value = jnp.dot(activated, w_second, preferred_element_type=jnp.float32).astype(jnp.bfloat16)
            part_sum = part_sum + partial_value.astype(jnp.float32)
        weighted = slot_weight[:, None] * part_sum
        running = running.at[safe_rows].add(weighted)
        return (running, None)
    running, _ = lax.scan(one_expert, jnp.zeros((ROWS, D), jnp.float32), jnp.arange(EXPERTS, dtype=jnp.int32))
    expert_hot = expert_ids[:, :, None] == jnp.arange(EXPERTS, dtype=jnp.int32)[None, None, :]
    expert_weight = lax.optimization_barrier(jnp.sum(jnp.where(expert_hot, route_weight[:, :, None], 0.0), axis=1))
    bias_term = jnp.dot(expert_weight, bias_out, precision=lax.Precision.HIGHEST)
    return (tok_float + running + bias_term).astype(jnp.bfloat16)
```

```python
import functools

import jax
import jax.numpy as jnp
from jax import lax
from jax.experimental import pallas as pl
from jax.experimental.pallas import tpu as pltpu
from jax.sharding import PartitionSpec as P

CAP = 18
PLANE = 4
LANES = 128
MESH = pl.DeviceIdType.MESH
VMEM_ROOM = 66_000_000


def round_up(value, step):
    return -(-value // step) * step


def expert_kernel(
    dims,
    normed_ref,
    meta_ref,
    pick_ref,
    gate_ref,
    mark_ref,
    inv_ref,
    weight_ref,
    bias_out_ref,
    bias_in_ref,
    w_in_ref,
    w_out_ref,
    out_ref,
    *scratch,
):
    depth, rows, width, half, slots, cols = dims
    count = len(cols)
    scratch = list(scratch)

    def take(n):
        got = scratch[:n]
        del scratch[:n]
        return got

    gathered = take(count)
    sending = take(count)
    landed = take(count)
    answers = take(count)
    from_above = take(count)
    from_below = take(count)
    (meta_all, select, combine, dense, acc, act, w_buf, w_out) = take(8)
    (w_sem, w_out_sem) = take(2)
    (up_send, down_send, chain_recv) = take(3)
    (side_send, side_recv, back_send, back_recv) = take(4)
    (ret_up_send, ret_down_send, ret_up_recv, ret_down_recv) = take(4)

    me = lax.axis_index("ep")
    level = me // PLANE
    seat = me % PLANE
    has_up = level < depth - 1
    has_down = level > 0
    starts = [sum(c for c, _ in cols[:k]) for k in range(count)]

    def w_copy(k):
        real = cols[k][1]
        return pltpu.make_async_copy(
            w_in_ref.at[0, pl.ds(starts[k], real), :],
            w_buf.at[k % 2, pl.ds(0, real), :],
            w_sem.at[k],
        )

    out_copy = pltpu.make_async_copy(w_out_ref.at[0], w_out, w_out_sem)
    w_copy(0).start()
    if count > 1:
        w_copy(1).start()
    out_copy.start()

    barrier = pltpu.get_barrier_semaphore()
    for step in range(1, PLANE):
        pl.semaphore_signal(
            barrier,
            inc=1,
            device_id={"ep": level * PLANE + lax.rem(seat + step, PLANE)},
            device_id_type=MESH,
        )

    @pl.when(has_up)
    def _():
        pl.semaphore_signal(barrier, inc=1, device_id={"ep": me + PLANE}, device_id_type=MESH)

    @pl.when(has_down)
    def _():
        pl.semaphore_signal(barrier, inc=1, device_id={"ep": me - PLANE}, device_id_type=MESH)

    peers = PLANE - 1 + has_up.astype(jnp.int32) + has_down.astype(jnp.int32)
    pl.semaphore_wait(barrier, peers)

    def block(k, z):
        buf = meta_all if k == 0 else gathered[k - 1]
        return buf.at[pl.ds(pl.multiple_of(z * rows, rows), rows), :]

    def chain(k, z, own, sem, target):
        if own:
            src = meta_ref if k == 0 else normed_ref.at[:, pl.ds(starts[k - 1], cols[k - 1][0])]
        else:
            src = block(k, z)
        return pltpu.make_async_remote_copy(
            src_ref=src,
            dst_ref=block(k, z),
            send_sem=sem.at[k, z],
            recv_sem=chain_recv.at[k, z],
            device_id={"ep": target},
            device_id_type=MESH,
        )

    def send_own(k):
        @pl.when(has_up)
        def _():
            chain(k, level, True, up_send, me + PLANE).start()

        @pl.when(has_down)
        def _():
            chain(k, level, True, down_send, me - PLANE).start()

    def relay(k):
        for far in range(1, depth):
            below = level - far

            @pl.when(below >= 0)
            def _():
                chain(k, below, False, up_send, me).wait_recv()

                @pl.when(has_up)
                def _():
                    chain(k, below, False, up_send, me + PLANE).start()

            above = level + far

            @pl.when(above < depth)
            def _():
                chain(k, above, False, down_send, me).wait_recv()

                @pl.when(has_down)
                def _():
                    chain(k, above, False, down_send, me - PLANE).start()

    def drain_chain(k):
        for z in range(depth):

            @pl.when(jnp.logical_and(has_up, z <= level))
            def _():
                chain(k, z, False, up_send, me + PLANE).wait_send()

            @pl.when(jnp.logical_and(has_down, z >= level))
            def _():
                chain(k, z, False, down_send, me - PLANE).wait_send()

    def seat_rows(buf, s):
        return buf.at[pl.ds(pl.multiple_of(s * slots, 16), slots), :]

    def side(k, step, src, dst, send, recv):
        peer = lax.rem(seat + step, PLANE)
        return pltpu.make_async_remote_copy(
            src_ref=seat_rows(src[k], peer),
            dst_ref=seat_rows(dst[k], seat),
            send_sem=send.at[k, step],
            recv_sem=recv.at[k, step],
            device_id={"ep": level * PLANE + peer},
            device_id_type=MESH,
        )

    def side_all(k, src, dst, send, recv):
        for step in range(1, PLANE):
            side(k, step, src, dst, send, recv).start()
        mine = pl.ds(pl.multiple_of(seat * slots, 16), slots)
        dst[k][mine, :] = src[k][mine, :]

    def first_matmul(k):
        real = cols[k][1]
        for step in range(1, PLANE):
            side(k, step, sending, landed, side_send, side_recv).wait_recv()
        w_copy(k).wait()
        x_ref = landed[k]

        def tile(start, size):
            part = jnp.dot(
                x_ref[:, :real],
                w_buf[k % 2, :real, pl.ds(start, size)],
                preferred_element_type=jnp.float32,
            )
            if k == 0:
                acc[:, pl.ds(start, size)] = part + bias_in_ref[:, pl.ds(start, size)]
            else:
                acc[:, pl.ds(start, size)] += part

        total = 2 * half
        size = 512
        full = total // size

        @pl.loop(0, full)
        def _(i):
            tile(pl.multiple_of(i * size, size), size)

        if total % size:
            tile(full * size, total % size)
        if k + 2 < count:
            w_copy(k + 2).start()

    send_own(0)
    send_own(1)
    own = pl.ds(pl.multiple_of(level * rows, rows), rows)
    meta_all[own, :] = meta_ref[...]
    for k in range(count):
        gathered[k][own, :] = normed_ref[:, starts[k] : starts[k] + cols[k][0]]
    relay(0)
    table = meta_all[...]
    rank = jnp.dot(table, pick_ref[...], preferred_element_type=jnp.float32)
    gate = jnp.dot(table, gate_ref[...], preferred_element_type=jnp.float32)
    hit = rank == mark_ref[...]
    combine[...] = jnp.where(hit, gate, 0.0).astype(jnp.bfloat16)
    select[...] = jnp.transpose(jnp.where(hit, 1.0, 0.0)).astype(jnp.bfloat16)

    for k in range(count):
        if k + 2 <= count:
            send_own(k + 2)
        relay(k + 1)
        sending[k][...] = jnp.dot(
            select[: PLANE * slots, :], gathered[k][...], preferred_element_type=jnp.float32
        ).astype(jnp.bfloat16)
        side_all(k, sending, landed, side_send, side_recv)
        if k > 0:
            first_matmul(k - 1)
    first_matmul(count - 1)

    part_rows = 32

    @pl.loop(0, PLANE * slots // part_rows)
    def _(i):
        here = pl.ds(pl.multiple_of(i * part_rows, part_rows), part_rows)
        for start in range(0, half, 384):
            size = min(384, half - start)
            g = acc[here, start : start + size]
            u = acc[here, half + start : half + start + size]
            act[here, start : start + size] = (
                g * jax.nn.sigmoid(1.702 * g) * (u + 1.0)
            ).astype(jnp.bfloat16)

    for k in range(count + 1):
        drain_chain(k)
    for k in range(count):
        for step in range(1, PLANE):
            side(k, step, sending, landed, side_send, side_recv).wait_send()
    out_copy.wait()

    def second_matmul(k):
        real = cols[k][1]
        size = 256

        def tile(start, at, n):
            sending[k][:, pl.ds(at, n)] = jnp.dot(
                act[...], w_out[:, pl.ds(start, n)], preferred_element_type=jnp.float32
            ).astype(jnp.bfloat16)

        full = real // size

        @pl.loop(0, full)
        def _(i):
            at = pl.multiple_of(i * size, size)
            tile(starts[k] + at, at, size)

        if real % size:
            tile(starts[k] + full * size, full * size, real % size)
        side_all(k, sending, answers, back_send, back_recv)

    def ret(k, z, land, send, recv, target):
        there = pl.ds(pl.multiple_of(z * rows, rows), rows)
        return pltpu.make_async_remote_copy(
            src_ref=gathered[k].at[there, :],
            dst_ref=land[k].at[there, :],
            send_sem=send.at[k, z],
            recv_sem=recv.at[k, z],
            device_id={"ep": target},
            device_id_type=MESH,
        )

    def pass_on(k, z, land, send, recv, target, more):
        there = pl.ds(z * rows, rows)

        @pl.when(more)
        def _():
            ret(k, z, land, send, recv, target).wait_recv()
            gathered[k][there, :] = (
                dense[there, : cols[k][0]] + land[k][there, :].astype(jnp.float32)
            ).astype(jnp.bfloat16)

        @pl.when(jnp.logical_not(more))
        def _():
            gathered[k][there, :] = dense[there, : cols[k][0]].astype(jnp.bfloat16)

        ret(k, z, land, send, recv, target).start()

    def reduce(k):
        for step in range(1, PLANE):
            side(k, step, sending, answers, back_send, back_recv).wait_recv()
        wide, real = cols[k]
        dense[:, :wide] = jnp.dot(
            combine[:, : PLANE * slots], answers[k][...], preferred_element_type=jnp.float32
        )
        for far in range(depth - 1):
            low, high = far, depth - 1 - far

            @pl.when(low < level)
            def _():
                pass_on(k, low, from_above, ret_down_send, ret_down_recv, me - PLANE, has_up)

            @pl.when(high > level)
            def _():
                pass_on(k, high, from_below, ret_up_send, ret_up_recv, me + PLANE, has_down)

    def finish(k):
        wide, real = cols[k]

        @pl.when(has_up)
        def _():
            ret(k, level, from_above, ret_down_send, ret_down_recv, me).wait_recv()

        @pl.when(has_down)
        def _():
            ret(k, level, from_below, ret_up_send, ret_up_recv, me).wait_recv()

        @pl.when(has_up)
        def _():
            home[k % 2, :, :wide] += from_above[k][own, :].astype(jnp.float32)

        @pl.when(has_down)
        def _():
            home[k % 2, :, :wide] += from_below[k][own, :].astype(jnp.float32)

        here = slice(starts[k], starts[k] + real)
        out_ref[:, here] = home[k % 2, :, :real] * inv_ref[...] + jnp.dot(
            weight_ref[...],
            bias_out_ref[:, here],
            preferred_element_type=jnp.float32,
            precision=lax.Precision.HIGHEST,
        )

    (home,) = take(1)
    for k in range(count):
        second_matmul(k)
        if k > 0:
            reduce(k - 1)
            home[(k - 1) % 2, :, : cols[k - 1][0]] = dense[own, : cols[k - 1][0]]
            if k > 1:
                finish(k - 2)
    last = count - 1
    reduce(last)
    home[last % 2, :, : cols[last][0]] = dense[own, : cols[last][0]]
    if last > 0:
        finish(last - 1)
    finish(last)

    for k in range(count):
        for step in range(1, PLANE):
            side(k, step, sending, answers, back_send, back_recv).wait_send()
        for z in range(depth):

            @pl.when(z < level)
            def _():
                ret(k, z, from_above, ret_down_send, ret_down_recv, me - PLANE).wait_send()

            @pl.when(z > level)
            def _():
                ret(k, z, from_below, ret_up_send, ret_up_recv, me + PLANE).wait_send()


def fused(tokens, expert_ids, gate_ints, norm_gain, weight_in, bias_in, weight_out, bias_out):
    size = lax.axis_size("ep")
    rows, width = tokens.shape
    experts = bias_out.shape[0]
    half = weight_out.shape[1]
    depth = size // PLANE
    slots = round_up(depth * CAP, 16)
    padded = round_up(width, LANES)
    cols = []
    while sum(c for c, _ in cols) < padded:
        at = sum(c for c, _ in cols)
        cols.append((min(768, padded - at), min(768, width - at)))
    cols = tuple(cols)
    count = len(cols)
    lane_slots = round_up(PLANE * slots, LANES)

    tok_float = tokens.astype(jnp.float32)
    row_scale = lax.rsqrt(jnp.mean(tok_float * tok_float, axis=1, keepdims=True) + 1e-05)
    normed = (tok_float * row_scale * norm_gain[None, :]).astype(jnp.bfloat16)
    normed = jnp.pad(normed, ((0, 0), (0, padded - width)))
    gates = gate_ints.astype(jnp.float32)
    inv = 1.0 / jnp.sum(gates, axis=1, keepdims=True)
    names = jnp.arange(experts, dtype=jnp.int32)
    hot = expert_ids[:, :, None] == names[None, None, :]
    chosen = jnp.any(hot, axis=1)
    gate_of = jnp.sum(jnp.where(hot, gates[:, :, None], 0.0), axis=1)
    expert_weight = gate_of * inv
    lower = jnp.tril(jnp.ones((rows, rows), jnp.bfloat16))
    rank = jnp.dot(lower, chosen.astype(jnp.bfloat16), preferred_element_type=jnp.float32)
    rank = jnp.where(chosen, rank, 0.0)
    gap = jnp.zeros((rows, LANES // 2 - experts), jnp.float32)
    meta = jnp.concatenate([rank, gap, gate_of, gap], axis=1).astype(jnp.bfloat16)

    level = lax.axis_index("ep") // PLANE
    slot = jnp.arange(lane_slots, dtype=jnp.int32)
    inside = slot % slots
    target = level * PLANE + slot // slots
    valid = (slot < PLANE * slots) & (inside < depth * CAP)
    lane = jnp.arange(LANES, dtype=jnp.int32)[:, None]
    pick = ((lane == target[None, :]) & valid[None, :]).astype(jnp.bfloat16)
    gate_pick = ((lane == LANES // 2 + target[None, :]) & valid[None, :]).astype(jnp.bfloat16)
    row_level = jnp.arange(depth * rows, dtype=jnp.int32)[:, None] // rows
    mark = jnp.where(
        valid[None, :] & (row_level == (inside // CAP)[None, :]),
        (inside % CAP + 1)[None, :],
        -1,
    ).astype(jnp.float32)

    bf16, f32 = jnp.bfloat16, jnp.float32
    all_rows, all_slots = depth * rows, PLANE * slots
    dma = pltpu.SemaphoreType.DMA

    def wide(n):
        return [pltpu.VMEM((n, c), bf16) for c, _ in cols]

    scratch = (
        wide(all_rows)
        + wide(all_slots)
        + wide(all_slots)
        + wide(all_slots)
        + wide(all_rows)
        + wide(all_rows)
        + [
            pltpu.VMEM((all_rows, LANES), bf16),
            pltpu.VMEM((lane_slots, all_rows), bf16),
            pltpu.VMEM((all_rows, lane_slots), bf16),
            pltpu.VMEM((all_rows, cols[0][0]), f32),
            pltpu.VMEM((all_slots, 2 * half), f32),
            pltpu.VMEM((all_slots, half), bf16),
            pltpu.VMEM((2, cols[0][0], 2 * half), bf16),
            pltpu.VMEM((half, width), bf16),
            dma((count,)),
            dma,
            dma((count + 1, depth)),
            dma((count + 1, depth)),
            dma((count + 1, depth)),
        ]
        + [dma((count, PLANE))] * 4
        + [dma((count, depth))] * 4
        + [pltpu.VMEM((2, rows, cols[0][0]), f32)]
    )
    vmem = pl.BlockSpec(memory_space=pltpu.VMEM)
    hbm = pl.BlockSpec(memory_space=pl.ANY)
    moe = pl.pallas_call(
        functools.partial(expert_kernel, (depth, rows, width, half, slots, cols)),
        out_shape=jax.ShapeDtypeStruct((rows, width), f32),
        in_specs=[vmem] * 9 + [hbm] * 2,
        out_specs=vmem,
        scratch_shapes=scratch,
        compiler_params=pltpu.CompilerParams(
            collective_id=0, has_side_effects=True, vmem_limit_bytes=VMEM_ROOM
        ),
    )(
        normed,
        meta,
        pick,
        gate_pick,
        mark,
        inv,
        expert_weight,
        bias_out,
        bias_in,
        weight_in,
        weight_out,
    )
    return (tok_float + moe).astype(jnp.bfloat16)


def shards(tokens, expert_ids, gate_ints, norm_gain, weight_in, bias_in, weight_out, bias_out):
    device_count = lax.axis_size("ep")
    expert_count = bias_out.shape[0]
    part_count = device_count // expert_count
    row_count, model_width = tokens.shape
    top_count = expert_ids.shape[1]
    capacity = CAP
    tok_float = tokens.astype(jnp.float32)
    row_scale = lax.rsqrt(jnp.mean(tok_float * tok_float, axis=1, keepdims=True) + 1e-05)
    normed = (tok_float * row_scale * norm_gain[None, :]).astype(jnp.bfloat16)
    int_gates = gate_ints.astype(jnp.float32)
    route_weight = int_gates / jnp.sum(int_gates, axis=1, keepdims=True)
    flat_ids = expert_ids.reshape(row_count * top_count)
    one_hot = (flat_ids[:, None] == jnp.arange(expert_count, dtype=jnp.int32)[None, :]).astype(
        jnp.int32
    )
    slot_rank = jnp.sum((jnp.cumsum(one_hot, axis=0) - one_hot) * one_hot, axis=1)
    slot_target = (flat_ids * capacity + slot_rank).reshape(row_count, top_count)
    slot_ids = jnp.arange(expert_count * capacity, dtype=jnp.int32)
    slot_match = slot_target[None, :, :] == slot_ids[:, None, None]
    picker = jnp.any(slot_match, axis=2).astype(jnp.bfloat16)
    placed = jnp.dot(picker, normed, preferred_element_type=jnp.float32).astype(jnp.bfloat16)
    combiner = jnp.transpose(jnp.sum(jnp.where(slot_match, route_weight[None, :, :], 0.0), axis=2))
    outgoing = jnp.broadcast_to(
        placed.reshape(expert_count, 1, capacity, model_width),
        (expert_count, part_count, capacity, model_width),
    ).reshape(device_count, capacity, model_width)
    arrived = lax.all_to_all(outgoing, "ep", split_axis=0, concat_axis=0, tiled=True)
    source_count = arrived.shape[0]
    slot_count = arrived.shape[1]
    flat_rows = arrived.reshape(source_count * slot_count, model_width)
    pre_act = (
        jnp.dot(flat_rows, weight_in[0], preferred_element_type=jnp.float32) + bias_in[0][None, :]
    )
    half_width = pre_act.shape[1] // 2
    gate_part = pre_act[:, :half_width]
    up_part = pre_act[:, half_width:]
    activated = (gate_part * jax.nn.sigmoid(1.702 * gate_part) * (up_part + 1.0)).astype(
        jnp.bfloat16
    )
    result = jnp.dot(activated, weight_out[0], preferred_element_type=jnp.float32).astype(
        jnp.bfloat16
    )
    returned = lax.all_to_all(
        result.reshape(source_count, slot_count, model_width),
        "ep",
        split_axis=0,
        concat_axis=0,
        tiled=True,
    )
    part_sum = jnp.sum(
        returned.reshape(expert_count, part_count, capacity, model_width), axis=1, dtype=jnp.float32
    ).reshape(expert_count * capacity, model_width)
    moe_rows = jnp.dot(combiner, part_sum, precision=lax.Precision.HIGHEST)
    expert_hot = expert_ids[:, :, None] == jnp.arange(expert_count, dtype=jnp.int32)[None, None, :]
    expert_weight = jnp.sum(jnp.where(expert_hot, route_weight[:, :, None], 0.0), axis=1)
    bias_term = jnp.dot(expert_weight, bias_out, precision=lax.Precision.HIGHEST)
    return (tok_float + moe_rows + bias_term).astype(jnp.bfloat16)


def layer(*arrays):
    weight_in, weight_out, bias_out = arrays[4], arrays[6], arrays[7]
    device_count = lax.axis_size("ep")
    one_each = device_count == bias_out.shape[0] and device_count % PLANE == 0
    held = 2 * weight_out.shape[1] * (2 * 2 * 768 + weight_out.shape[2])
    if one_each and 2 * held < 3 * VMEM_ROOM and bias_out.shape[0] <= LANES // 2:
        return fused(*arrays)
    return shards(*arrays)


def solution(mesh):
    return jax.shard_map(
        layer,
        mesh=mesh,
        in_specs=(
            P(("groups", "ep"), None),
            P(("groups", "ep"), None),
            P(("groups", "ep"), None),
            P(),
            P("ep", None, None),
            P("ep", None),
            P("ep", None, None),
            P(),
        ),
        out_specs=P(("groups", "ep"), None),
        check_vma=False,
    )
```

```python
import functools

import jax
import jax.numpy as jnp
import numpy as np
from jax import lax
from jax.experimental import pallas as pl
from jax.experimental.pallas import tpu as pltpu
from jax.sharding import PartitionSpec as P

CAP = 18
PLANE = 4
LANES = 128
MESH = pl.DeviceIdType.MESH
VMEM_ROOM = 66_000_000


def round_up(value, step):
    return -(-value // step) * step


def expert_kernel(
    dims,
    tokens_ref,
    ids_ref,
    gates_ref,
    gain_ref,
    slot_ref,
    bias_out_ref,
    bias_in_ref,
    w_in_ref,
    w_out_ref,
    out_ref,
    *scratch,
):
    depth, rows, width, half, slots, cols = dims
    count = len(cols)
    scratch = list(scratch)

    def take(n):
        got = scratch[:n]
        del scratch[:n]
        return got

    gathered = take(count)
    sending = take(count)
    landed = take(count)
    answers = take(count)
    relayed = take(count)
    home_in = take(count)
    (meta_all, select, combine, dense, acc, act, w_buf, w_out) = take(8)
    (normed_ref, meta_ref) = take(2)
    (w_sem, w_out_sem) = take(2)
    (own_send, pass_send, chain_recv) = take(3)
    (side_send, side_recv, back_send, back_recv) = take(4)
    (ret_send, ret_recv, home_recv) = take(3)

    me = lax.axis_index("ep")
    level = me // PLANE
    seat = me % PLANE
    has_up = level < depth - 1
    has_down = level > 0
    near = [(d - 1, level + d < depth, me + d * PLANE) for d in (2, 1) if d < depth]
    near += [(d + 1, level - d >= 0, me - d * PLANE) for d in (2, 1) if d < depth]
    starts = [sum(c for c, _ in cols[:k]) for k in range(count)]

    def w_copy(k):
        real = cols[k][1]
        return pltpu.make_async_copy(
            w_in_ref.at[0, pl.ds(starts[k], real), :],
            w_buf.at[k % 2, pl.ds(0, real), :],
            w_sem.at[k],
        )

    out_copy = pltpu.make_async_copy(w_out_ref.at[0], w_out, w_out_sem)
    w_copy(0).start()
    if count > 1:
        w_copy(1).start()

    barrier = pltpu.get_barrier_semaphore()
    for step in range(1, PLANE):
        pl.semaphore_signal(
            barrier,
            inc=1,
            device_id={"ep": level * PLANE + lax.rem(seat + step, PLANE)},
            device_id_type=MESH,
        )

    peers = PLANE - 1
    for _, present, device in near:
        peers = peers + present.astype(jnp.int32)

        @pl.when(present)
        def _():
            pl.semaphore_signal(barrier, inc=1, device_id={"ep": device}, device_id_type=MESH)

    bf16, f32 = jnp.bfloat16, jnp.float32
    experts = bias_out_ref.shape[0]
    lane = lax.broadcasted_iota(jnp.int32, (rows, LANES), 1)
    gates = gates_ref[...].astype(f32)
    inv = 1.0 / jnp.sum(gates, axis=1, keepdims=True)
    chosen = jnp.zeros((rows, LANES), f32)
    gate_of = jnp.zeros((rows, LANES), f32)
    gate_lane = jnp.zeros((rows, LANES), f32)
    for entry in range(ids_ref.shape[1]):
        name = ids_ref[:, entry : entry + 1]
        value = gates[:, entry : entry + 1]
        chosen += jnp.where(lane == name, 1.0, 0.0)
        gate_of += jnp.where(lane == name, value, 0.0)
        gate_lane += jnp.where(lane == name + LANES // 2, value, 0.0)
    lower = jnp.where(
        lax.broadcasted_iota(jnp.int32, (rows, rows), 0)
        >= lax.broadcasted_iota(jnp.int32, (rows, rows), 1),
        1.0,
        0.0,
    ).astype(bf16)
    rank = jnp.dot(lower, chosen.astype(bf16), preferred_element_type=f32)
    meta_ref[...] = (rank * chosen + gate_lane).astype(bf16)
    tok = tokens_ref[...].astype(f32)
    scale = lax.rsqrt(jnp.sum(tok * tok, axis=1, keepdims=True) * (1.0 / width) + 1e-05)
    normed_ref[:, :width] = (tok * scale * gain_ref[...]).astype(bf16)
    if normed_ref.shape[1] > width:
        normed_ref[:, width:] = jnp.zeros((rows, normed_ref.shape[1] - width), bf16)
    pl.semaphore_wait(barrier, peers)

    def block(k, z):
        buf = meta_all if k == 0 else gathered[k - 1]
        return buf.at[pl.ds(pl.multiple_of(z * rows, rows), rows), :]

    def chain(k, z, own, sem, at, target):
        if own:
            src = meta_ref if k == 0 else normed_ref.at[:, pl.ds(starts[k - 1], cols[k - 1][0])]
        else:
            src = block(k, z)
        return pltpu.make_async_remote_copy(
            src_ref=src,
            dst_ref=block(k, z),
            send_sem=sem.at[k, at],
            recv_sem=chain_recv.at[k, z],
            device_id={"ep": target},
            device_id_type=MESH,
        )

    def send_own(k):
        for slot, present, device in near:

            @pl.when(present)
            def _():
                chain(k, level, True, own_send, slot, device).start()

    def relay(k):
        for far in [*range(2, depth), 1]:
            for z, on, device in (
                (level - far, has_up, me + PLANE),
                (level + far, has_down, me - PLANE),
            ):

                @pl.when(jnp.logical_and(z >= 0, z < depth))
                def _():
                    chain(k, z, False, pass_send, z, me).wait_recv()
                    if far > 1:

                        @pl.when(on)
                        def _():
                            chain(k, z, False, pass_send, z, device).start()

    def drain_chain(k):
        for slot, present, device in near:

            @pl.when(present)
            def _():
                chain(k, level, True, own_send, slot, device).wait_send()

        for z in range(depth):

            @pl.when(jnp.logical_or(has_up & (z <= level - 2), has_down & (z >= level + 2)))
            def _():
                chain(k, z, False, pass_send, z, me).wait_send()

    def seat_rows(buf, s):
        return buf.at[pl.ds(pl.multiple_of(s * slots, 16), slots), :]

    def side(k, step, src, dst, send, recv):
        peer = lax.rem(seat + step, PLANE)
        return pltpu.make_async_remote_copy(
            src_ref=seat_rows(src[k], peer),
            dst_ref=seat_rows(dst[k], seat),
            send_sem=send.at[k, step],
            recv_sem=recv.at[k, step],
            device_id={"ep": level * PLANE + peer},
            device_id_type=MESH,
        )

    def side_all(k, src, dst, send, recv):
        for step in range(1, PLANE):
            side(k, step, src, dst, send, recv).start()
        mine = pl.ds(pl.multiple_of(seat * slots, 16), slots)
        dst[k][mine, :] = src[k][mine, :]

    def first_matmul(k):
        real = cols[k][1]
        for step in range(1, PLANE):
            side(k, step, sending, landed, side_send, side_recv).wait_recv()
        w_copy(k).wait()
        x_ref = landed[k]

        def tile(start, size):
            part = jnp.dot(
                x_ref[:, :real],
                w_buf[k % 2, :real, pl.ds(start, size)],
                preferred_element_type=jnp.float32,
            )
            if k == 0:
                acc[:, pl.ds(start, size)] = part + bias_in_ref[:, pl.ds(start, size)]
            else:
                acc[:, pl.ds(start, size)] += part

        total = 2 * half
        size = 512
        full = total // size

        @pl.loop(0, full)
        def _(i):
            tile(pl.multiple_of(i * size, size), size)

        if total % size:
            tile(full * size, total % size)
        if k + 2 < count:
            w_copy(k + 2).start()
        if k == 0:
            out_copy.start()

    send_own(0)
    send_own(1)
    send_own(2)
    own = pl.ds(pl.multiple_of(level * rows, rows), rows)
    meta_all[own, :] = meta_ref[...]
    for k in range(count):
        gathered[k][own, :] = normed_ref[:, starts[k] : starts[k] + cols[k][0]]
    targets = slot_ref[0:1, :] + (level * PLANE).astype(f32)
    sub = lax.broadcasted_iota(jnp.int32, (LANES, slot_ref.shape[1]), 0).astype(f32)
    pick = jnp.where(sub == targets, 1.0, 0.0).astype(bf16)
    gate_pick = jnp.where(sub == targets + LANES // 2, 1.0, 0.0).astype(bf16)
    relay(0)
    table = meta_all[...]
    rank = jnp.dot(table, pick, preferred_element_type=f32)
    gate = jnp.dot(table, gate_pick, preferred_element_type=f32)
    for z in range(depth):
        there = slice(z * rows, (z + 1) * rows)
        hit = (rank[there, :] == slot_ref[2:3, :]) & (slot_ref[1:2, :] == z)
        combine[there, :] = jnp.where(hit, gate[there, :], 0.0).astype(bf16)
        dense[there, : slot_ref.shape[1]] = jnp.where(hit, 1.0, 0.0)
    select[...] = jnp.transpose(dense[:, : slot_ref.shape[1]]).astype(bf16)

    for k in range(count):
        if k + 3 <= count:
            send_own(k + 3)
        relay(k + 1)
        sending[k][...] = jnp.dot(
            select[: PLANE * slots, :], gathered[k][...], preferred_element_type=jnp.float32
        ).astype(jnp.bfloat16)
        side_all(k, sending, landed, side_send, side_recv)
        if k > 0:
            first_matmul(k - 1)
    first_matmul(count - 1)

    part_rows = 32

    @pl.loop(0, PLANE * slots // part_rows)
    def _(i):
        here = pl.ds(pl.multiple_of(i * part_rows, part_rows), part_rows)
        for start in range(0, half, 384):
            size = min(384, half - start)
            g = acc[here, start : start + size]
            u = acc[here, half + start : half + start + size]
            act[here, start : start + size] = (
                g * jax.nn.sigmoid(1.702 * g) * (u + 1.0)
            ).astype(jnp.bfloat16)

    for k in range(count + 1):
        drain_chain(k)
    for k in range(count):
        for step in range(1, PLANE):
            side(k, step, sending, landed, side_send, side_recv).wait_send()
    out_copy.wait()

    def second_matmul(k):
        real = cols[k][1]
        size = 256

        def tile(start, at, n):
            sending[k][:, pl.ds(at, n)] = jnp.dot(
                act[...], w_out[:, pl.ds(start, n)], preferred_element_type=jnp.float32
            ).astype(jnp.bfloat16)

        full = real // size

        @pl.loop(0, full)
        def _(i):
            at = pl.multiple_of(i * size, size)
            tile(starts[k] + at, at, size)

        if real % size:
            tile(starts[k] + full * size, full * size, real % size)
        side_all(k, sending, answers, back_send, back_recv)

    def rows_of(z):
        return pl.ds(pl.multiple_of(z * rows, rows), rows)

    def ret(k, z, slot, target):
        if slot is None:
            dst, recv = relayed[k].at[rows_of(z), :], ret_recv.at[k, z]
        else:
            dst, recv = home_in[k].at[pl.ds(slot * rows, rows), :], home_recv.at[k, slot]
        return pltpu.make_async_remote_copy(
            src_ref=gathered[k].at[rows_of(z), :],
            dst_ref=dst,
            send_sem=ret_send.at[k, z],
            recv_sem=recv,
            device_id={"ep": target},
            device_id_type=MESH,
        )

    def pass_on(k, z, far, more, slot, target):
        there = rows_of(z)
        wide = cols[k][0]
        if far > 1:

            @pl.when(more)
            def _():
                ret(k, z, None, me).wait_recv()
                gathered[k][there, :] = (
                    dense[there, :wide] + relayed[k][there, :].astype(jnp.float32)
                ).astype(jnp.bfloat16)

            @pl.when(jnp.logical_not(more))
            def _():
                gathered[k][there, :] = dense[there, :wide].astype(jnp.bfloat16)

        else:
            gathered[k][there, :] = dense[there, :wide].astype(jnp.bfloat16)
        ret(k, z, slot, target).start()

    def reduce(k):
        for step in range(1, PLANE):
            side(k, step, sending, answers, back_send, back_recv).wait_recv()
        wide, real = cols[k]
        dense[:, :wide] = jnp.dot(
            combine[:, : PLANE * slots], answers[k][...], preferred_element_type=jnp.float32
        )
        for far in [*range(depth - 1, 2, -1), 1, 2]:
            if far >= depth:
                continue
            low, high = level - far, level + far

            @pl.when(low >= 0)
            def _():
                direct = far <= 2
                hop = far if direct else 1
                pass_on(k, low, far, has_up, far - 1 if direct else None, me - hop * PLANE)

            @pl.when(high < depth)
            def _():
                direct = far <= 2
                hop = far if direct else 1
                pass_on(k, high, far, has_down, far + 1 if direct else None, me + hop * PLANE)

    def finish(k):
        wide, real = cols[k]

        for slot, present, device in near:

            @pl.when(present)
            def _():
                ret(k, level, slot, me).wait_recv()
                home[k % 2, :, :wide] += home_in[k][slot * rows : (slot + 1) * rows, :].astype(
                    jnp.float32
                )

        here = slice(starts[k], starts[k] + real)
        moe = home[k % 2, :, :real] * inv + jnp.dot(
            (gate_of * inv)[:, :experts],
            bias_out_ref[:, here],
            preferred_element_type=f32,
            precision=lax.Precision.HIGHEST,
        )
        out_ref[:, here] = (tokens_ref[:, here].astype(f32) + moe).astype(bf16)

    (home,) = take(1)
    for k in range(count):
        second_matmul(k)
        if k > 0:
            reduce(k - 1)
            home[(k - 1) % 2, :, : cols[k - 1][0]] = dense[own, : cols[k - 1][0]]
            if k > 1:
                finish(k - 2)
    last = count - 1
    reduce(last)
    home[last % 2, :, : cols[last][0]] = dense[own, : cols[last][0]]
    if last > 0:
        finish(last - 1)
    finish(last)

    for k in range(count):
        for step in range(1, PLANE):
            side(k, step, sending, answers, back_send, back_recv).wait_send()
        for z in range(depth):

            @pl.when(z != level)
            def _():
                ret(k, z, None, me).wait_send()


def fused(tokens, expert_ids, gate_ints, norm_gain, weight_in, bias_in, weight_out, bias_out):
    size = lax.axis_size("ep")
    rows, width = tokens.shape
    experts = bias_out.shape[0]
    half = weight_out.shape[1]
    depth = size // PLANE
    slots = round_up(depth * CAP, 16)
    padded = round_up(width, LANES)
    cols = []
    while sum(c for c, _ in cols) < padded:
        at = sum(c for c, _ in cols)
        cols.append((min(768, padded - at), min(768, width - at)))
    cols = tuple(cols)
    count = len(cols)
    lane_slots = round_up(PLANE * slots, LANES)

    table = np.full((8, lane_slots), -1000.0, np.float32)
    for slot in range(PLANE * slots):
        inside = slot % slots
        if inside < depth * CAP:
            table[:3, slot] = (slot // slots, inside // CAP, inside % CAP + 1)

    bf16, f32 = jnp.bfloat16, jnp.float32
    all_rows, all_slots = depth * rows, PLANE * slots
    dma = pltpu.SemaphoreType.DMA

    def wide(n):
        return [pltpu.VMEM((n, c), bf16) for c, _ in cols]

    scratch = (
        wide(all_rows)
        + wide(all_slots)
        + wide(all_slots)
        + wide(all_slots)
        + wide(all_rows)
        + wide(4 * rows)
        + [
            pltpu.VMEM((all_rows, LANES), bf16),
            pltpu.VMEM((lane_slots, all_rows), bf16),
            pltpu.VMEM((all_rows, lane_slots), bf16),
            pltpu.VMEM((all_rows, cols[0][0]), f32),
            pltpu.VMEM((all_slots, 2 * half), f32),
            pltpu.VMEM((all_slots, half), bf16),
            pltpu.VMEM((2, cols[0][0], 2 * half), bf16),
            pltpu.VMEM((half, width), bf16),
            pltpu.VMEM((rows, padded), bf16),
            pltpu.VMEM((rows, LANES), bf16),
            dma((count,)),
            dma,
            dma((count + 1, 4)),
            dma((count + 1, depth)),
            dma((count + 1, depth)),
        ]
        + [dma((count, PLANE))] * 4
        + [dma((count, depth)), dma((count, depth)), dma((count, 4))]
        + [pltpu.VMEM((2, rows, cols[0][0]), f32)]
    )
    vmem = pl.BlockSpec(memory_space=pltpu.VMEM)
    hbm = pl.BlockSpec(memory_space=pl.ANY)
    return pl.pallas_call(
        functools.partial(expert_kernel, (depth, rows, width, half, slots, cols)),
        out_shape=jax.ShapeDtypeStruct((rows, width), bf16),
        in_specs=[vmem] * 7 + [hbm] * 2,
        out_specs=vmem,
        scratch_shapes=scratch,
        compiler_params=pltpu.CompilerParams(
            collective_id=0, has_side_effects=True, vmem_limit_bytes=VMEM_ROOM
        ),
    )(
        tokens,
        expert_ids,
        gate_ints,
        norm_gain.reshape(1, width),
        jnp.asarray(table),
        bias_out,
        bias_in,
        weight_in,
        weight_out,
    )


def shards(tokens, expert_ids, gate_ints, norm_gain, weight_in, bias_in, weight_out, bias_out):
    device_count = lax.axis_size("ep")
    expert_count = bias_out.shape[0]
    part_count = device_count // expert_count
    row_count, model_width = tokens.shape
    top_count = expert_ids.shape[1]
    capacity = CAP
    tok_float = tokens.astype(jnp.float32)
    row_scale = lax.rsqrt(jnp.mean(tok_float * tok_float, axis=1, keepdims=True) + 1e-05)
    normed = (tok_float * row_scale * norm_gain[None, :]).astype(jnp.bfloat16)
    int_gates = gate_ints.astype(jnp.float32)
    route_weight = int_gates / jnp.sum(int_gates, axis=1, keepdims=True)
    flat_ids = expert_ids.reshape(row_count * top_count)
    one_hot = (flat_ids[:, None] == jnp.arange(expert_count, dtype=jnp.int32)[None, :]).astype(
        jnp.int32
    )
    slot_rank = jnp.sum((jnp.cumsum(one_hot, axis=0) - one_hot) * one_hot, axis=1)
    slot_target = (flat_ids * capacity + slot_rank).reshape(row_count, top_count)
    slot_ids = jnp.arange(expert_count * capacity, dtype=jnp.int32)
    slot_match = slot_target[None, :, :] == slot_ids[:, None, None]
    picker = jnp.any(slot_match, axis=2).astype(jnp.bfloat16)
    placed = jnp.dot(picker, normed, preferred_element_type=jnp.float32).astype(jnp.bfloat16)
    combiner = jnp.transpose(jnp.sum(jnp.where(slot_match, route_weight[None, :, :], 0.0), axis=2))
    outgoing = jnp.broadcast_to(
        placed.reshape(expert_count, 1, capacity, model_width),
        (expert_count, part_count, capacity, model_width),
    ).reshape(device_count, capacity, model_width)
    arrived = lax.all_to_all(outgoing, "ep", split_axis=0, concat_axis=0, tiled=True)
    source_count = arrived.shape[0]
    slot_count = arrived.shape[1]
    flat_rows = arrived.reshape(source_count * slot_count, model_width)
    pre_act = (
        jnp.dot(flat_rows, weight_in[0], preferred_element_type=jnp.float32) + bias_in[0][None, :]
    )
    half_width = pre_act.shape[1] // 2
    gate_part = pre_act[:, :half_width]
    up_part = pre_act[:, half_width:]
    activated = (gate_part * jax.nn.sigmoid(1.702 * gate_part) * (up_part + 1.0)).astype(
        jnp.bfloat16
    )
    result = jnp.dot(activated, weight_out[0], preferred_element_type=jnp.float32).astype(
        jnp.bfloat16
    )
    returned = lax.all_to_all(
        result.reshape(source_count, slot_count, model_width),
        "ep",
        split_axis=0,
        concat_axis=0,
        tiled=True,
    )
    part_sum = jnp.sum(
        returned.reshape(expert_count, part_count, capacity, model_width), axis=1, dtype=jnp.float32
    ).reshape(expert_count * capacity, model_width)
    moe_rows = jnp.dot(combiner, part_sum, precision=lax.Precision.HIGHEST)
    expert_hot = expert_ids[:, :, None] == jnp.arange(expert_count, dtype=jnp.int32)[None, None, :]
    expert_weight = jnp.sum(jnp.where(expert_hot, route_weight[:, :, None], 0.0), axis=1)
    bias_term = jnp.dot(expert_weight, bias_out, precision=lax.Precision.HIGHEST)
    return (tok_float + moe_rows + bias_term).astype(jnp.bfloat16)


def layer(*arrays):
    weight_in, weight_out, bias_out = arrays[4], arrays[6], arrays[7]
    device_count = lax.axis_size("ep")
    one_each = device_count == bias_out.shape[0] and device_count % PLANE == 0
    held = 2 * weight_out.shape[1] * (2 * 2 * 768 + weight_out.shape[2])
    if one_each and 2 * held < 3 * VMEM_ROOM and bias_out.shape[0] <= LANES // 2:
        return fused(*arrays)
    return shards(*arrays)


def solution(mesh):
    return jax.shard_map(
        layer,
        mesh=mesh,
        in_specs=(
            P(("groups", "ep"), None),
            P(("groups", "ep"), None),
            P(("groups", "ep"), None),
            P(),
            P("ep", None, None),
            P("ep", None),
            P("ep", None, None),
            P(),
        ),
        out_specs=P(("groups", "ep"), None),
        check_vma=False,
    )
```

```python
import functools

import jax
import jax.numpy as jnp
import numpy as np
from jax import lax
from jax.experimental import pallas as pl
from jax.experimental.pallas import tpu as pltpu
from jax.sharding import PartitionSpec as P

CAP = 18
PLANE = 4
LANES = 128
MESH = pl.DeviceIdType.MESH
VMEM_ROOM = 66_000_000


def round_up(value, step):
    return -(-value // step) * step


def expert_kernel(
    dims,
    tokens_ref,
    ids_ref,
    gates_ref,
    gain_ref,
    slot_ref,
    bias_out_ref,
    bias_in_ref,
    w_in_ref,
    w_out_ref,
    out_ref,
    *scratch,
):
    depth, rows, width, half, slots, cols = dims
    count = len(cols)
    scratch = list(scratch)

    def take(n):
        got = scratch[:n]
        del scratch[:n]
        return got

    gathered = take(count)
    sending = take(count)
    landed = take(count)
    answers = take(count)
    relayed = take(count)
    home_in = take(count)
    (meta_all, select, combine, dense, acc, act, w_buf, w_out) = take(8)
    (normed_ref, meta_ref) = take(2)
    (w_sem, w_out_sem) = take(2)
    (own_send, pass_send, chain_recv) = take(3)
    (side_send, side_recv, back_send, back_recv) = take(4)
    (ret_send, ret_recv, home_recv) = take(3)

    me = lax.axis_index("ep")
    level = me // PLANE
    seat = me % PLANE
    has_up = level < depth - 1
    has_down = level > 0
    near = [(d - 1, level + d < depth, me + d * PLANE) for d in (2, 1) if d < depth]
    near += [(d + 1, level - d >= 0, me - d * PLANE) for d in (2, 1) if d < depth]
    starts = [sum(c for c, _ in cols[:k]) for k in range(count)]

    def w_copy(k):
        real = cols[k][1]
        return pltpu.make_async_copy(
            w_in_ref.at[0, pl.ds(starts[k], real), :],
            w_buf.at[k % 2, pl.ds(0, real), :],
            w_sem.at[k],
        )

    out_copy = pltpu.make_async_copy(w_out_ref.at[0], w_out, w_out_sem)
    w_copy(0).start()
    if count > 1:
        w_copy(1).start()

    barrier = pltpu.get_barrier_semaphore()
    for step in range(1, PLANE):
        pl.semaphore_signal(
            barrier,
            inc=1,
            device_id={"ep": level * PLANE + lax.rem(seat + step, PLANE)},
            device_id_type=MESH,
        )

    peers = PLANE - 1
    for _, present, device in near:
        peers = peers + present.astype(jnp.int32)

        @pl.when(present)
        def _():
            pl.semaphore_signal(barrier, inc=1, device_id={"ep": device}, device_id_type=MESH)

    bf16, f32 = jnp.bfloat16, jnp.float32
    experts = bias_out_ref.shape[0]
    lane = lax.broadcasted_iota(jnp.int32, (rows, LANES), 1)
    gates = gates_ref[...].astype(f32)
    inv = 1.0 / jnp.sum(gates, axis=1, keepdims=True)
    chosen = jnp.zeros((rows, LANES), f32)
    gate_of = jnp.zeros((rows, LANES), f32)
    gate_lane = jnp.zeros((rows, LANES), f32)
    for entry in range(ids_ref.shape[1]):
        name = ids_ref[:, entry : entry + 1]
        value = gates[:, entry : entry + 1]
        chosen += jnp.where(lane == name, 1.0, 0.0)
        gate_of += jnp.where(lane == name, value, 0.0)
        gate_lane += jnp.where(lane == name + LANES // 2, value, 0.0)
    lower = jnp.where(
        lax.broadcasted_iota(jnp.int32, (rows, rows), 0)
        >= lax.broadcasted_iota(jnp.int32, (rows, rows), 1),
        1.0,
        0.0,
    ).astype(bf16)
    rank = jnp.dot(lower, chosen.astype(bf16), preferred_element_type=f32)
    meta_ref[...] = (rank * chosen + gate_lane).astype(bf16)
    tok = tokens_ref[...].astype(f32)
    scale = lax.rsqrt(jnp.sum(tok * tok, axis=1, keepdims=True) * (1.0 / width) + 1e-05)
    normed_ref[:, :width] = (tok * scale * gain_ref[...]).astype(bf16)
    if normed_ref.shape[1] > width:
        normed_ref[:, width:] = jnp.zeros((rows, normed_ref.shape[1] - width), bf16)
    pl.semaphore_wait(barrier, peers)

    def block(k, z):
        buf = meta_all if k == 0 else gathered[k - 1]
        return buf.at[pl.ds(pl.multiple_of(z * rows, rows), rows), :]

    def chain(k, z, own, sem, at, target):
        if own:
            src = meta_ref if k == 0 else normed_ref.at[:, pl.ds(starts[k - 1], cols[k - 1][0])]
        else:
            src = block(k, z)
        return pltpu.make_async_remote_copy(
            src_ref=src,
            dst_ref=block(k, z),
            send_sem=sem.at[k, at],
            recv_sem=chain_recv.at[k, z],
            device_id={"ep": target},
            device_id_type=MESH,
        )

    def send_own(k):
        for slot, present, device in near:

            @pl.when(present)
            def _():
                chain(k, level, True, own_send, slot, device).start()

    def relay(k):
        for far in [*range(2, depth), 1]:
            for z, on, device in (
                (level - far, has_up, me + PLANE),
                (level + far, has_down, me - PLANE),
            ):

                @pl.when(jnp.logical_and(z >= 0, z < depth))
                def _():
                    chain(k, z, False, pass_send, z, me).wait_recv()
                    if far > 1:

                        @pl.when(on)
                        def _():
                            chain(k, z, False, pass_send, z, device).start()

    def drain_chain(k):
        for slot, present, device in near:

            @pl.when(present)
            def _():
                chain(k, level, True, own_send, slot, device).wait_send()

        for z in range(depth):

            @pl.when(jnp.logical_or(has_up & (z <= level - 2), has_down & (z >= level + 2)))
            def _():
                chain(k, z, False, pass_send, z, me).wait_send()

    def seat_rows(buf, s):
        return buf.at[pl.ds(pl.multiple_of(s * slots, 16), slots), :]

    def side(k, step, src, dst, send, recv):
        peer = lax.rem(seat + step, PLANE)
        return pltpu.make_async_remote_copy(
            src_ref=seat_rows(src[k], peer),
            dst_ref=seat_rows(dst[k], seat),
            send_sem=send.at[k, step],
            recv_sem=recv.at[k, step],
            device_id={"ep": level * PLANE + peer},
            device_id_type=MESH,
        )

    def side_all(k, src, dst, send, recv):
        for step in range(1, PLANE):
            side(k, step, src, dst, send, recv).start()
        mine = pl.ds(pl.multiple_of(seat * slots, 16), slots)
        dst[k][mine, :] = src[k][mine, :]

    def first_matmul(k):
        real = cols[k][1]
        for step in range(1, PLANE):
            side(k, step, sending, landed, side_send, side_recv).wait_recv()
        w_copy(k).wait()
        x_ref = landed[k]

        def tile(start, size):
            part = jnp.dot(
                x_ref[:, :real],
                w_buf[k % 2, :real, pl.ds(start, size)],
                preferred_element_type=jnp.float32,
            )
            if k == 0:
                acc[:, pl.ds(start, size)] = part + bias_in_ref[:, pl.ds(start, size)]
            else:
                acc[:, pl.ds(start, size)] += part

        total = 2 * half
        size = 1152
        full = total // size

        @pl.loop(0, full)
        def _(i):
            tile(pl.multiple_of(i * size, size), size)

        if total % size:
            tile(full * size, total % size)
        if k + 2 < count:
            w_copy(k + 2).start()
        if k == 0:
            out_copy.start()

    send_own(0)
    send_own(1)
    send_own(2)
    own = pl.ds(pl.multiple_of(level * rows, rows), rows)
    meta_all[own, :] = meta_ref[...]
    for k in range(count):
        gathered[k][own, :] = normed_ref[:, starts[k] : starts[k] + cols[k][0]]
    targets = slot_ref[0:1, :] + (level * PLANE).astype(f32)
    sub = lax.broadcasted_iota(jnp.int32, (LANES, slot_ref.shape[1]), 0).astype(f32)
    pick = jnp.where(sub == targets, 1.0, 0.0).astype(bf16)
    gate_pick = jnp.where(sub == targets + LANES // 2, 1.0, 0.0).astype(bf16)
    relay(0)
    table = meta_all[...]
    rank = jnp.dot(table, pick, preferred_element_type=f32)
    gate = jnp.dot(table, gate_pick, preferred_element_type=f32)
    for z in range(depth):
        there = slice(z * rows, (z + 1) * rows)
        hit = (rank[there, :] == slot_ref[2:3, :]) & (slot_ref[1:2, :] == z)
        combine[there, :] = jnp.where(hit, gate[there, :], 0.0).astype(bf16)
        dense[there, : slot_ref.shape[1]] = jnp.where(hit, 1.0, 0.0)
    select[...] = jnp.transpose(dense[:, : slot_ref.shape[1]]).astype(bf16)

    for k in range(count):
        if k + 3 <= count:
            send_own(k + 3)
        relay(k + 1)
        sending[k][...] = jnp.dot(
            select[: PLANE * slots, :], gathered[k][...], preferred_element_type=jnp.float32
        ).astype(jnp.bfloat16)
        side_all(k, sending, landed, side_send, side_recv)
        if k > 0:
            first_matmul(k - 1)
    first_matmul(count - 1)

    part_rows = 32

    @pl.loop(0, PLANE * slots // part_rows)
    def _(i):
        here = pl.ds(pl.multiple_of(i * part_rows, part_rows), part_rows)
        for start in range(0, half, 384):
            size = min(384, half - start)
            g = acc[here, start : start + size]
            u = acc[here, half + start : half + start + size]
            act[here, start : start + size] = (
                g * jax.nn.sigmoid(1.702 * g) * (u + 1.0)
            ).astype(jnp.bfloat16)

    for k in range(count + 1):
        drain_chain(k)
    for k in range(count):
        for step in range(1, PLANE):
            side(k, step, sending, landed, side_send, side_recv).wait_send()
    out_copy.wait()

    def second_matmul(k):
        real = cols[k][1]
        size = 256

        def tile(start, at, n):
            sending[k][:, pl.ds(at, n)] = jnp.dot(
                act[...], w_out[:, pl.ds(start, n)], preferred_element_type=jnp.float32
            ).astype(jnp.bfloat16)

        full = real // size

        @pl.loop(0, full)
        def _(i):
            at = pl.multiple_of(i * size, size)
            tile(starts[k] + at, at, size)

        if real % size:
            tile(starts[k] + full * size, full * size, real % size)
        side_all(k, sending, answers, back_send, back_recv)

    def rows_of(z):
        return pl.ds(pl.multiple_of(z * rows, rows), rows)

    def ret(k, z, slot, target):
        if slot is None:
            dst, recv = relayed[k].at[rows_of(z), :], ret_recv.at[k, z]
        else:
            dst, recv = home_in[k].at[pl.ds(slot * rows, rows), :], home_recv.at[k, slot]
        return pltpu.make_async_remote_copy(
            src_ref=gathered[k].at[rows_of(z), :],
            dst_ref=dst,
            send_sem=ret_send.at[k, z],
            recv_sem=recv,
            device_id={"ep": target},
            device_id_type=MESH,
        )

    def pass_on(k, z, far, more, slot, target):
        there = rows_of(z)
        wide = cols[k][0]
        if far > 1:

            @pl.when(more)
            def _():
                ret(k, z, None, me).wait_recv()
                gathered[k][there, :] = (
                    dense[there, :wide] + relayed[k][there, :].astype(jnp.float32)
                ).astype(jnp.bfloat16)

            @pl.when(jnp.logical_not(more))
            def _():
                gathered[k][there, :] = dense[there, :wide].astype(jnp.bfloat16)

        else:
            gathered[k][there, :] = dense[there, :wide].astype(jnp.bfloat16)
        ret(k, z, slot, target).start()

    def reduce(k):
        for step in range(1, PLANE):
            side(k, step, sending, answers, back_send, back_recv).wait_recv()
        wide, real = cols[k]
        dense[:, :wide] = jnp.dot(
            combine[:, : PLANE * slots], answers[k][...], preferred_element_type=jnp.float32
        )
        for far in [*range(depth - 1, 2, -1), 1, 2]:
            if far >= depth:
                continue
            low, high = level - far, level + far

            @pl.when(low >= 0)
            def _():
                direct = far <= 2
                hop = far if direct else 1
                pass_on(k, low, far, has_up, far - 1 if direct else None, me - hop * PLANE)

            @pl.when(high < depth)
            def _():
                direct = far <= 2
                hop = far if direct else 1
                pass_on(k, high, far, has_down, far + 1 if direct else None, me + hop * PLANE)

    def finish(k):
        wide, real = cols[k]

        for slot, present, device in near:

            @pl.when(present)
            def _():
                ret(k, level, slot, me).wait_recv()
                home[k % 2, :, :wide] += home_in[k][slot * rows : (slot + 1) * rows, :].astype(
                    jnp.float32
                )

        here = slice(starts[k], starts[k] + real)
        moe = home[k % 2, :, :real] * inv + jnp.dot(
            (gate_of * inv)[:, :experts],
            bias_out_ref[:, here],
            preferred_element_type=f32,
            precision=lax.Precision.HIGHEST,
        )
        out_ref[:, here] = (tokens_ref[:, here].astype(f32) + moe).astype(bf16)

    (home,) = take(1)
    for k in range(count):
        second_matmul(k)
        if k > 0:
            reduce(k - 1)
            home[(k - 1) % 2, :, : cols[k - 1][0]] = dense[own, : cols[k - 1][0]]
            if k > 1:
                finish(k - 2)
    last = count - 1
    reduce(last)
    home[last % 2, :, : cols[last][0]] = dense[own, : cols[last][0]]
    if last > 0:
        finish(last - 1)
    finish(last)

    for k in range(count):
        for step in range(1, PLANE):
            side(k, step, sending, answers, back_send, back_recv).wait_send()
        for z in range(depth):

            @pl.when(z != level)
            def _():
                ret(k, z, None, me).wait_send()


def fused(tokens, expert_ids, gate_ints, norm_gain, weight_in, bias_in, weight_out, bias_out):
    size = lax.axis_size("ep")
    rows, width = tokens.shape
    experts = bias_out.shape[0]
    half = weight_out.shape[1]
    depth = size // PLANE
    slots = round_up(depth * CAP, 16)
    padded = round_up(width, LANES)
    cols = []
    while sum(c for c, _ in cols) < padded:
        at = sum(c for c, _ in cols)
        cols.append((min(768, padded - at), min(768, width - at)))
    cols = tuple(cols)
    count = len(cols)
    lane_slots = round_up(PLANE * slots, LANES)

    table = np.full((8, lane_slots), -1000.0, np.float32)
    for slot in range(PLANE * slots):
        inside = slot % slots
        if inside < depth * CAP:
            table[:3, slot] = (slot // slots, inside // CAP, inside % CAP + 1)

    bf16, f32 = jnp.bfloat16, jnp.float32
    all_rows, all_slots = depth * rows, PLANE * slots
    dma = pltpu.SemaphoreType.DMA

    def wide(n):
        return [pltpu.VMEM((n, c), bf16) for c, _ in cols]

    scratch = (
        wide(all_rows)
        + wide(all_slots)
        + wide(all_slots)
        + wide(all_slots)
        + wide(all_rows)
        + wide(4 * rows)
        + [
            pltpu.VMEM((all_rows, LANES), bf16),
            pltpu.VMEM((lane_slots, all_rows), bf16),
            pltpu.VMEM((all_rows, lane_slots), bf16),
            pltpu.VMEM((all_rows, cols[0][0]), f32),
            pltpu.VMEM((all_slots, 2 * half), f32),
            pltpu.VMEM((all_slots, half), bf16),
            pltpu.VMEM((2, cols[0][0], 2 * half), bf16),
            pltpu.VMEM((half, width), bf16),
            pltpu.VMEM((rows, padded), bf16),
            pltpu.VMEM((rows, LANES), bf16),
            dma((count,)),
            dma,
            dma((count + 1, 4)),
            dma((count + 1, depth)),
            dma((count + 1, depth)),
        ]
        + [dma((count, PLANE))] * 4
        + [dma((count, depth)), dma((count, depth)), dma((count, 4))]
        + [pltpu.VMEM((2, rows, cols[0][0]), f32)]
    )
    vmem = pl.BlockSpec(memory_space=pltpu.VMEM)
    hbm = pl.BlockSpec(memory_space=pl.ANY)
    return pl.pallas_call(
        functools.partial(expert_kernel, (depth, rows, width, half, slots, cols)),
        out_shape=jax.ShapeDtypeStruct((rows, width), bf16),
        in_specs=[vmem] * 7 + [hbm] * 2,
        out_specs=vmem,
        scratch_shapes=scratch,
        compiler_params=pltpu.CompilerParams(
            collective_id=0, has_side_effects=True, vmem_limit_bytes=VMEM_ROOM
        ),
    )(
        tokens,
        expert_ids,
        gate_ints,
        norm_gain.reshape(1, width),
        jnp.asarray(table),
        bias_out,
        bias_in,
        weight_in,
        weight_out,
    )


def shards(tokens, expert_ids, gate_ints, norm_gain, weight_in, bias_in, weight_out, bias_out):
    device_count = lax.axis_size("ep")
    expert_count = bias_out.shape[0]
    part_count = device_count // expert_count
    row_count, model_width = tokens.shape
    top_count = expert_ids.shape[1]
    capacity = CAP
    tok_float = tokens.astype(jnp.float32)
    row_scale = lax.rsqrt(jnp.mean(tok_float * tok_float, axis=1, keepdims=True) + 1e-05)
    normed = (tok_float * row_scale * norm_gain[None, :]).astype(jnp.bfloat16)
    int_gates = gate_ints.astype(jnp.float32)
    route_weight = int_gates / jnp.sum(int_gates, axis=1, keepdims=True)
    flat_ids = expert_ids.reshape(row_count * top_count)
    one_hot = (flat_ids[:, None] == jnp.arange(expert_count, dtype=jnp.int32)[None, :]).astype(
        jnp.int32
    )
    slot_rank = jnp.sum((jnp.cumsum(one_hot, axis=0) - one_hot) * one_hot, axis=1)
    slot_target = (flat_ids * capacity + slot_rank).reshape(row_count, top_count)
    slot_ids = jnp.arange(expert_count * capacity, dtype=jnp.int32)
    slot_match = slot_target[None, :, :] == slot_ids[:, None, None]
    picker = jnp.any(slot_match, axis=2).astype(jnp.bfloat16)
    placed = jnp.dot(picker, normed, preferred_element_type=jnp.float32).astype(jnp.bfloat16)
    combiner = jnp.transpose(jnp.sum(jnp.where(slot_match, route_weight[None, :, :], 0.0), axis=2))
    outgoing = jnp.broadcast_to(
        placed.reshape(expert_count, 1, capacity, model_width),
        (expert_count, part_count, capacity, model_width),
    ).reshape(device_count, capacity, model_width)
    arrived = lax.all_to_all(outgoing, "ep", split_axis=0, concat_axis=0, tiled=True)
    source_count = arrived.shape[0]
    slot_count = arrived.shape[1]
    flat_rows = arrived.reshape(source_count * slot_count, model_width)
    pre_act = (
        jnp.dot(flat_rows, weight_in[0], preferred_element_type=jnp.float32) + bias_in[0][None, :]
    )
    half_width = pre_act.shape[1] // 2
    gate_part = pre_act[:, :half_width]
    up_part = pre_act[:, half_width:]
    activated = (gate_part * jax.nn.sigmoid(1.702 * gate_part) * (up_part + 1.0)).astype(
        jnp.bfloat16
    )
    result = jnp.dot(activated, weight_out[0], preferred_element_type=jnp.float32).astype(
        jnp.bfloat16
    )
    returned = lax.all_to_all(
        result.reshape(source_count, slot_count, model_width),
        "ep",
        split_axis=0,
        concat_axis=0,
        tiled=True,
    )
    part_sum = jnp.sum(
        returned.reshape(expert_count, part_count, capacity, model_width), axis=1, dtype=jnp.float32
    ).reshape(expert_count * capacity, model_width)
    moe_rows = jnp.dot(combiner, part_sum, precision=lax.Precision.HIGHEST)
    expert_hot = expert_ids[:, :, None] == jnp.arange(expert_count, dtype=jnp.int32)[None, None, :]
    expert_weight = jnp.sum(jnp.where(expert_hot, route_weight[:, :, None], 0.0), axis=1)
    bias_term = jnp.dot(expert_weight, bias_out, precision=lax.Precision.HIGHEST)
    return (tok_float + moe_rows + bias_term).astype(jnp.bfloat16)


def layer(*arrays):
    weight_in, weight_out, bias_out = arrays[4], arrays[6], arrays[7]
    device_count = lax.axis_size("ep")
    one_each = device_count == bias_out.shape[0] and device_count % PLANE == 0
    held = 2 * weight_out.shape[1] * (2 * 2 * 768 + weight_out.shape[2])
    if one_each and 2 * held < 3 * VMEM_ROOM and bias_out.shape[0] <= LANES // 2:
        return fused(*arrays)
    return shards(*arrays)


def solution(mesh):
    return jax.shard_map(
        layer,
        mesh=mesh,
        in_specs=(
            P(("groups", "ep"), None),
            P(("groups", "ep"), None),
            P(("groups", "ep"), None),
            P(),
            P("ep", None, None),
            P("ep", None),
            P("ep", None, None),
            P(),
        ),
        out_specs=P(("groups", "ep"), None),
        check_vma=False,
    )
```
